32 devices in a mesh: region: 4 (over x, core), sector: 8 (over z, y).
Axes of the slice: x: 2, y: 2, z: 4, core: 2. Of those that a mesh axis runs over, the one named last changes fastest.
Arguments:
- env_left: bfloat16 [4, 8, 2048, 2048], P('region', None, 'sector'), may hold values from -6 to 6
- site_tensor: bfloat16 [4, 2048, 2, 2048], P('region', 'sector'), may hold values from -0.125 to 0.125
- mpo_tensor: float32 [4, 8, 8, 2, 2], P('region'), may hold values from -1 to 1
- env_right: bfloat16 [4, 8, 2048, 2048], P('region', None, 'sector'), may hold values from -0.046875 to 0.046875
- bond_tensor: bfloat16 [4, 2048, 2048], P('region'), may hold values from -0.125 to 0.125
Outputs:
- env_next: bfloat16 [4, 8, 2048, 2048], P('region', None, 'sector')
- bond_image: bfloat16 [4, 2048, 2048], P('region', 'sector')
The draws below stay inside these ranges and needn't reach their ends.
All inputs are finite; a program needn't handle non-finite values.
Results may differ from the reference program's by a relative error of at most 0.0065.
Values may be sent and summed in bfloat16 or wider, within the bound.
A program may use at most 192 MiB of HBM per device.

```python
import jax
import jax.numpy as jnp
from jax import lax

CHI = 2048
W = 8
D_PHYS = 2
NREG = 4
N_REGION = 4


def level_of(own_key, dims, split, least, top_value):
    def one(position, shards_of):
        steps = jax.random.uniform(jax.random.fold_in(jax.random.fold_in(own_key, 6), position), (shards_of,), jnp.float32, least / len(split), top_value / len(split))
        return jnp.repeat(jnp.exp(steps), dims[position] // shards_of).reshape((-1,) + (1,) * (len(dims) - position - 1))

    factor_of = one(*split[0])
    for cut in split[1:]:
        factor_of = factor_of * one(*cut)
    return factor_of


def gaussian(rng, dims, scale, most, shards=(), dtype=jnp.bfloat16):
    values = jax.random.normal(rng, dims, jnp.float32) * scale
    if len(shards) > 0:
        values = level_of(rng, dims, shards, -0.22, 0.18) * values
    return jnp.clip(values, min=-most, max=most).astype(dtype)


def setup_inputs(seed: int = 0) -> dict:
    arg_keys = jax.random.split(jax.random.key(seed), 6)
    env_left = gaussian(arg_keys[0], (NREG, W, CHI, CHI), 1.0, 6.0, ((0, 4), (2, 8)))
    site_tensor = gaussian(arg_keys[1], (NREG, CHI, D_PHYS, CHI), CHI ** -0.5, 0.125, ((0, 4), (1, 8)))
    mpo_tensor = gaussian(arg_keys[2], (NREG, W, W, D_PHYS, D_PHYS), (W * D_PHYS * D_PHYS) ** -0.5, 1.0, ((0, 4),), jnp.float32)
    env_right = gaussian(arg_keys[3], (NREG, W, CHI, CHI), (CHI * W) ** -0.5, 0.046875, ((0, 4), (2, 8)))
    bond_tensor = gaussian(arg_keys[4], (NREG, CHI, CHI), CHI ** -0.5, 0.125, ((0, 4),))
    return dict(env_left=env_left, site_tensor=site_tensor, mpo_tensor=mpo_tensor, env_right=env_right, bond_tensor=bond_tensor)


def reference(env_left, site_tensor, mpo_tensor, env_right, bond_tensor):
    env_list = []
    image_list = []
    for region_id in range(N_REGION):
        site_whole = site_tensor[region_id].astype(jnp.float32)
        half_done = jnp.einsum("wak,ksc->wasc", env_left[region_id].astype(jnp.float32), site_whole)
        carried = jnp.einsum("vwst,vatc->wsac", mpo_tensor[region_id], half_done, precision=lax.Precision.HIGHEST).astype(jnp.bfloat16)
        env_new = jnp.einsum("wsac,asb->wcb", carried.astype(jnp.float32), site_whole).astype(jnp.bfloat16)
        right_next = env_right[(region_id + 1) % N_REGION].astype(jnp.float32)
        bond_right = jnp.einsum("wbc,kc->wbk", right_next, bond_tensor[region_id].astype(jnp.float32)).astype(jnp.bfloat16)
        image_new = jnp.einsum("wka,wbk->ab", env_new.astype(jnp.float32), bond_right.astype(jnp.float32)).astype(jnp.bfloat16)
        env_list.append(env_new)
        image_list.append(image_new)
    return jnp.stack(env_list), jnp.stack(image_list)
```

```python
import functools

import jax
import jax.numpy as jnp
from jax import lax
from jax.experimental import pallas as pl
from jax.experimental.pallas import tpu as pltpu
from jax.sharding import PartitionSpec as P


GROUP = 16
LANES = 128
CHUNKS = 2
VMEM_LIMIT = 60 * 1024 * 1024


def shifted(block, axis, distance):
    devices = range(lax.axis_size(axis))
    route = [((i - distance) % len(devices), i) for i in devices]
    return lax.ppermute(block, axis, route)


def swap(blocks):
    return lax.all_to_all(blocks, "sector", split_axis=0, concat_axis=0, tiled=True)


def carried_kernel(mix_ref, env_ref, site_ref, *out_refs):
    width, rows, bond = env_ref.shape
    _, states, _, columns = site_ref.shape
    mix = mix_ref[...]
    mix_high = mix.astype(jnp.bfloat16)
    mix_low = (mix - mix_high.astype(jnp.float32)).astype(jnp.bfloat16)
    env = env_ref[...].reshape(width * rows, bond)
    half_done = [
        jnp.dot(env, site_ref[:, t].reshape(bond, columns), preferred_element_type=jnp.float32)
        .reshape(width, rows, columns)
        for t in range(states)
    ]
    dot = functools.partial(jnp.dot, preferred_element_type=jnp.float32)
    for g in range(rows // GROUP):
        span = slice(g * GROUP, (g + 1) * GROUP)
        x = jnp.concatenate(
            [h[:, span].reshape(width * GROUP, columns) for h in half_done], axis=0
        )
        high = x.astype(jnp.bfloat16)
        low = (x - high.astype(jnp.float32)).astype(jnp.bfloat16)
        y = dot(mix_high, high) + dot(mix_high, low) + dot(mix_low, high)
        y = y.astype(jnp.bfloat16).reshape(width, states, GROUP, columns)
        step = width // len(out_refs)
        for i, out_ref in enumerate(out_refs):
            out_ref[0, :, :, span, :] = y[i * step : (i + 1) * step]


def carried_blocks(env_left, gathered, mpo, row_tile):
    width, rows, bond = env_left.shape
    parts, states, depth, _ = gathered.shape
    columns = bond // parts
    eye = jnp.eye(GROUP, dtype=jnp.float32)
    side = width * states * GROUP
    mix = jnp.einsum("vwst,ij->wsitvj", mpo, eye, precision=lax.Precision.HIGHEST).reshape(side, side)
    step = width // CHUNKS
    out = jax.ShapeDtypeStruct((parts, step, states, rows, columns), jnp.bfloat16)
    return pl.pallas_call(
        carried_kernel,
        grid=(rows // row_tile, parts),
        in_specs=[
            pl.BlockSpec((side, side), lambda i, j: (0, 0)),
            pl.BlockSpec((width, row_tile, bond), lambda i, j: (0, i, 0)),
            pl.BlockSpec((parts, states, depth, columns), lambda i, j: (0, 0, 0, j)),
        ],
        out_specs=[
            pl.BlockSpec((1, step, states, row_tile, columns), lambda i, j: (j, 0, 0, i, 0))
        ] * CHUNKS,
        out_shape=[out] * CHUNKS,
        compiler_params=pltpu.CompilerParams(vmem_limit_bytes=VMEM_LIMIT),
        cost_estimate=pl.CostEstimate(
            flops=2 * width * rows * bond * bond * states,
            bytes_accessed=96 * 1024 * 1024,
            transcendentals=0,
        ),
    )(mix, env_left, gathered)


def env_kernel(x_ref, site_ref, *rest):
    out_ref, turned = rest[-2:]
    parts, count, states, depth, columns = x_ref.shape

    @pl.when(pl.program_id(0) == 0)
    def _():
        for n in range(parts):
            for s in range(states):
                at = (n * states + s) * depth
                for v in range(count):
                    turned[v * columns : (v + 1) * columns, at : at + depth] = x_ref[n, v, s].T

    site = site_ref[...].reshape(parts * states * depth, site_ref.shape[-1])
    total = jnp.dot(turned[...], site, preferred_element_type=jnp.float32)
    out_ref[...] = total.astype(jnp.bfloat16).reshape(out_ref.shape)


def env_chunk(moved, gathered, previous, chunk, width, tile):
    parts, count, states, depth, columns = moved.shape
    bond = gathered.shape[-1]
    operands = (moved, gathered) + (() if previous is None else (previous,))
    specs = [
        pl.BlockSpec(moved.shape, lambda j: (0, 0, 0, 0, 0), pipeline_mode=pl.Buffered(1)),
        pl.BlockSpec((parts, states, depth, tile), lambda j: (0, 0, 0, j)),
    ]
    if previous is not None:
        specs.append(pl.BlockSpec(memory_space=pl.ANY))
    return pl.pallas_call(
        env_kernel,
        grid=(bond // tile,),
        in_specs=specs,
        out_specs=pl.BlockSpec((count, columns, tile), lambda j: (chunk, 0, j)),
        out_shape=jax.ShapeDtypeStruct((width, columns, bond), jnp.bfloat16),
        scratch_shapes=[pltpu.VMEM((count * columns, parts * states * depth), jnp.bfloat16)],
        input_output_aliases={} if previous is None else {2: 0},
        compiler_params=pltpu.CompilerParams(vmem_limit_bytes=VMEM_LIMIT),
        cost_estimate=pl.CostEstimate(
            flops=2 * count * columns * parts * states * depth * bond,
            bytes_accessed=32 * 1024 * 1024,
            transcendentals=0,
        ),
    )(*operands)


def local(env_left, site_tensor, mpo_tensor, env_right, bond_tensor):
    parts = lax.axis_size("sector")
    width, rows, bond = env_left.shape[1:]
    columns = bond // parts
    gathered = lax.all_gather(site_tensor[0].transpose(1, 0, 2), "sector", axis=0)
    right_next = shifted(env_right, "region", -1)[0]
    bond_blocks = jnp.einsum(
        "dkc,wbc->dwkb",
        bond_tensor[0].reshape(parts, columns, bond),
        right_next,
        preferred_element_type=jnp.float32,
    ).astype(jnp.bfloat16)
    bond_blocks, gathered = lax.optimization_barrier((bond_blocks, gathered))
    bond_moved = swap(bond_blocks)
    carried = carried_blocks(env_left[0], gathered, mpo_tensor[0], min(rows, LANES))
    moved = []
    for i in range(CHUNKS):
        moved.append(swap(carried[i]))
    env_new = None
    for i in range(CHUNKS):
        env_new = env_chunk(moved[i], gathered, env_new, i, width, 2 * LANES)
    image = jnp.einsum(
        "wka,nwkb->anb", env_new, bond_moved, preferred_element_type=jnp.float32
    ).astype(jnp.bfloat16).reshape(bond, bond)
    image_rows = lax.psum_scatter(image, "sector", scatter_dimension=0, tiled=True)
    return (env_new[None], image_rows[None])


def plain_local(env_left, site_tensor, mpo_tensor, env_right, bond_tensor):
    width = env_left.shape[1]
    states = site_tensor.shape[2]
    gathered = lax.all_gather(site_tensor, "sector", axis=1, tiled=True)[0]
    half_done = jnp.einsum(
        "wak,ksc->wasc", env_left[0], gathered, preferred_element_type=jnp.float32
    )
    carried = jnp.einsum(
        "vwst,vatc->wsac", mpo_tensor[0], half_done, precision=lax.Precision.HIGHEST
    ).astype(jnp.bfloat16)
    carried = carried.reshape((width * states,) + carried.shape[2:])
    right_next = shifted(env_right, "region", -1)[0]
    bond_right = jnp.einsum(
        "wbc,kc->wbk", right_next, bond_tensor[0], preferred_element_type=jnp.float32
    ).astype(jnp.bfloat16)
    carried_moved = lax.all_to_all(carried, "sector", split_axis=2, concat_axis=1, tiled=True)
    bond_moved = lax.all_to_all(bond_right, "sector", split_axis=2, concat_axis=1, tiled=True)
    carried_moved = carried_moved.reshape((width, states) + carried_moved.shape[1:])
    env_new = jnp.einsum(
        "wsac,asb->wcb", carried_moved, gathered, preferred_element_type=jnp.float32
    ).astype(jnp.bfloat16)
    image_rows = lax.psum_scatter(
        jnp.einsum("wka,wbk->ab", env_new, bond_moved, preferred_element_type=jnp.float32),
        "sector",
        scatter_dimension=0,
        tiled=True,
    )
    return (env_new[None], image_rows.astype(jnp.bfloat16)[None])


def solution(mesh):
    def body(env_left, site_tensor, mpo_tensor, env_right, bond_tensor):
        width, rows, bond = env_left.shape[1:]
        columns = bond // mesh.shape["sector"]
        tiled = rows % LANES == 0 and columns % LANES == 0 and width % CHUNKS == 0
        step = local if tiled else plain_local
        return step(env_left, site_tensor, mpo_tensor, env_right, bond_tensor)

    return jax.shard_map(
        body,
        mesh=mesh,
        in_specs=(
            P("region", None, "sector", None),
            P("region", "sector", None, None),
            P("region", None, None, None, None),
            P("region", None, "sector", None),
            P("region", None, None),
        ),
        out_specs=(P("region", None, "sector", None), P("region", "sector", None)),
        check_vma=False,
    )
```

```python
import functools

import jax
import jax.numpy as jnp
from jax import lax
from jax.experimental import pallas as pl
from jax.experimental.pallas import tpu as pltpu
from jax.sharding import PartitionSpec as P


GROUP = 16
LANES = 128
CHUNKS = 2
VMEM_LIMIT = 60 * 1024 * 1024


def shifted(block, axis, distance):
    devices = range(lax.axis_size(axis))
    route = [((i - distance) % len(devices), i) for i in devices]
    return lax.ppermute(block, axis, route)


def swap(blocks):
    return lax.all_to_all(blocks, "sector", split_axis=0, concat_axis=0, tiled=True)


def carried_kernel(mix_ref, env_ref, site_ref, *out_refs):
    width, rows, bond = env_ref.shape
    _, states, _, columns = site_ref.shape
    mix = mix_ref[...]
    mix_high = mix.astype(jnp.bfloat16)
    mix_low = (mix - mix_high.astype(jnp.float32)).astype(jnp.bfloat16)
    env = env_ref[...].reshape(width * rows, bond)
    half_done = [
        jnp.dot(env, site_ref[:, t].reshape(bond, columns), preferred_element_type=jnp.float32)
        .reshape(width, rows, columns)
        for t in range(states)
    ]
    dot = functools.partial(jnp.dot, preferred_element_type=jnp.float32)
    for g in range(rows // GROUP):
        span = slice(g * GROUP, (g + 1) * GROUP)
        x = jnp.concatenate(
            [h[:, span].reshape(width * GROUP, columns) for h in half_done], axis=0
        )
        high = x.astype(jnp.bfloat16)
        low = (x - high.astype(jnp.float32)).astype(jnp.bfloat16)
        y = dot(mix_high, high) + dot(mix_high, low) + dot(mix_low, high)
        y = y.astype(jnp.bfloat16).reshape(width, states, GROUP, columns)
        step = width // len(out_refs)
        for i, out_ref in enumerate(out_refs):
            out_ref[0, :, :, span, :] = y[i * step : (i + 1) * step]


def carried_blocks(env_left, gathered, mpo, row_tile):
    width, rows, bond = env_left.shape
    parts, states, depth, _ = gathered.shape
    columns = bond // parts
    eye = jnp.eye(GROUP, dtype=jnp.float32)
    side = width * states * GROUP
    mix = jnp.einsum("vwst,ij->wsitvj", mpo, eye, precision=lax.Precision.HIGHEST).reshape(side, side)
    step = width // CHUNKS
    out = jax.ShapeDtypeStruct((parts, step, states, rows, columns), jnp.bfloat16)
    return pl.pallas_call(
        carried_kernel,
        grid=(rows // row_tile, parts),
        in_specs=[
            pl.BlockSpec((side, side), lambda i, j: (0, 0)),
            pl.BlockSpec((width, row_tile, bond), lambda i, j: (0, i, 0)),
            pl.BlockSpec((parts, states, depth, columns), lambda i, j: (0, 0, 0, j)),
        ],
        out_specs=[
            pl.BlockSpec((1, step, states, row_tile, columns), lambda i, j: (j, 0, 0, i, 0))
        ] * CHUNKS,
        out_shape=[out] * CHUNKS,
        compiler_params=pltpu.CompilerParams(vmem_limit_bytes=VMEM_LIMIT),
        cost_estimate=pl.CostEstimate(
            flops=2 * width * rows * bond * bond * states,
            bytes_accessed=96 * 1024 * 1024,
            transcendentals=0,
        ),
    )(mix, env_left, gathered)


def env_kernel(x_ref, site_ref, *rest):
    out_ref, turned = rest[-2:]
    parts, count, states, depth, columns = x_ref.shape

    @pl.when(pl.program_id(0) == 0)
    def _():
        for n in range(parts):
            for s in range(states):
                at = (n * states + s) * depth
                for v in range(count):
                    turned[v * columns : (v + 1) * columns, at : at + depth] = x_ref[n, v, s].T

    site = site_ref[...].reshape(parts * states * depth, site_ref.shape[-1])
    total = jnp.dot(turned[...], site, preferred_element_type=jnp.float32)
    out_ref[...] = total.astype(jnp.bfloat16).reshape(out_ref.shape)


def env_chunk(moved, gathered, previous, chunk, width, tile):
    parts, count, states, depth, columns = moved.shape
    bond = gathered.shape[-1]
    operands = (moved, gathered) + (() if previous is None else (previous,))
    specs = [
        pl.BlockSpec(moved.shape, lambda j: (0, 0, 0, 0, 0), pipeline_mode=pl.Buffered(1)),
        pl.BlockSpec((parts, states, depth, tile), lambda j: (0, 0, 0, j)),
    ]
    if previous is not None:
        specs.append(pl.BlockSpec(memory_space=pl.ANY))
    return pl.pallas_call(
        env_kernel,
        grid=(bond // tile,),
        in_specs=specs,
        out_specs=pl.BlockSpec((count, columns, tile), lambda j: (chunk, 0, j)),
        out_shape=jax.ShapeDtypeStruct((width, columns, bond), jnp.bfloat16),
        scratch_shapes=[pltpu.VMEM((count * columns, parts * states * depth), jnp.bfloat16)],
        input_output_aliases={} if previous is None else {2: 0},
        compiler_params=pltpu.CompilerParams(vmem_limit_bytes=VMEM_LIMIT),
        cost_estimate=pl.CostEstimate(
            flops=2 * count * columns * parts * states * depth * bond,
            bytes_accessed=32 * 1024 * 1024,
            transcendentals=0,
        ),
    )(*operands)


def local(env_left, site_tensor, mpo_tensor, env_right, bond_tensor):
    parts = lax.axis_size("sector")
    width, rows, bond = env_left.shape[1:]
    columns = bond // parts
    half = rows // CHUNKS
    gathered = lax.all_gather(site_tensor[0].transpose(1, 0, 2), "sector", axis=0)
    right_next = shifted(env_right, "region", -1)[0]
    bond_blocks = []
    for i in range(CHUNKS):
        blocks = jnp.einsum(
            "dkc,wbc->dwkb",
            bond_tensor[0].reshape(parts, columns, bond),
            right_next[:, i * half : (i + 1) * half],
            preferred_element_type=jnp.float32,
        )
        bond_blocks.append(blocks.astype(jnp.bfloat16))
    bond_moved = []
    for i in range(CHUNKS):
        bond_moved.append(swap(bond_blocks[i]))
    carried = carried_blocks(env_left[0], gathered, mpo_tensor[0], min(rows, LANES))
    moved = []
    for i in range(CHUNKS):
        moved.append(swap(carried[i]))
    env_new = None
    for i in range(CHUNKS):
        env_new = env_chunk(moved[i], gathered, env_new, i, width, 2 * LANES)
    image_rows = []
    for i in range(CHUNKS):
        image = jnp.einsum(
            "wkda,nwkb->dnba",
            env_new.reshape(width, columns, parts, columns),
            bond_moved[i],
            preferred_element_type=jnp.float32,
        ).astype(jnp.bfloat16).reshape(parts, parts * half, columns)
        image_rows.append(lax.psum_scatter(image, "sector", scatter_dimension=0, tiled=False))
    image_rows = jnp.stack(
        [x.reshape(parts, half, columns) for x in image_rows], axis=1
    ).reshape(bond, columns).T
    return (env_new[None], image_rows[None])


def plain_local(env_left, site_tensor, mpo_tensor, env_right, bond_tensor):
    width = env_left.shape[1]
    states = site_tensor.shape[2]
    gathered = lax.all_gather(site_tensor, "sector", axis=1, tiled=True)[0]
    half_done = jnp.einsum(
        "wak,ksc->wasc", env_left[0], gathered, preferred_element_type=jnp.float32
    )
    carried = jnp.einsum(
        "vwst,vatc->wsac", mpo_tensor[0], half_done, precision=lax.Precision.HIGHEST
    ).astype(jnp.bfloat16)
    carried = carried.reshape((width * states,) + carried.shape[2:])
    right_next = shifted(env_right, "region", -1)[0]
    bond_right = jnp.einsum(
        "wbc,kc->wbk", right_next, bond_tensor[0], preferred_element_type=jnp.float32
    ).astype(jnp.bfloat16)
    carried_moved = lax.all_to_all(carried, "sector", split_axis=2, concat_axis=1, tiled=True)
    bond_moved = lax.all_to_all(bond_right, "sector", split_axis=2, concat_axis=1, tiled=True)
    carried_moved = carried_moved.reshape((width, states) + carried_moved.shape[1:])
    env_new = jnp.einsum(
        "wsac,asb->wcb", carried_moved, gathered, preferred_element_type=jnp.float32
    ).astype(jnp.bfloat16)
    image_rows = lax.psum_scatter(
        jnp.einsum("wka,wbk->ab", env_new, bond_moved, preferred_element_type=jnp.float32),
        "sector",
        scatter_dimension=0,
        tiled=True,
    )
    return (env_new[None], image_rows.astype(jnp.bfloat16)[None])


def solution(mesh):
    def body(env_left, site_tensor, mpo_tensor, env_right, bond_tensor):
        width, rows, bond = env_left.shape[1:]
        columns = bond // mesh.shape["sector"]
        tiled = rows % LANES == 0 and columns % LANES == 0 and width % CHUNKS == 0
        step = local if tiled else plain_local
        return step(env_left, site_tensor, mpo_tensor, env_right, bond_tensor)

    return jax.shard_map(
        body,
        mesh=mesh,
        in_specs=(
            P("region", None, "sector", None),
            P("region", "sector", None, None),
            P("region", None, None, None, None),
            P("region", None, "sector", None),
            P("region", None, None),
        ),
        out_specs=(P("region", None, "sector", None), P("region", "sector", None)),
        check_vma=False,
    )
```
